32 devices in a mesh: replica: 2 (over y), section: 2 (over core), seq: 8 (over z, x).
Axes of the slice: x: 2, y: 2, z: 4, core: 2. Of those that a mesh axis runs over, the one named last changes fastest.
Arguments:
- latents: float32 [2, 1024, 64], P('section', ('replica', 'seq')), parts along dimension 1, may hold values from -6 to 6
- cond: bfloat16 [2, 3, 1024, 4096], P('section', None, ('replica', 'seq')), parts along dimension 2, may hold values from -60 to 60
- embed: bfloat16 [2, 3, 64, 4096], P('section'), may hold values from -0.75 to 0.75
- audio_table: bfloat16 [2, 64, 4096], P('section', 'replica'), parts along dimension 1, may hold values from -6 to 6
- audio_map: int32 [64], P(('replica', 'seq')), parts along dimension 0, may hold values from 0 to 31
- out_proj: bfloat16 [2, 4096, 64], P('section'), may hold values from -0.5 to 0.5
- tile_start: int32 [16], P('replica'), parts along dimension 0, may hold values 0 or 1
- conv_input: bfloat16 [3, 3, 16, 512], P(None, None, None, 'section'), may hold values from -0.5 to 0.5
- conv_first: bfloat16 [3, 3, 512, 512], P(None, None, None, 'section'), may hold values from -0.09375 to 0.09375
- conv_second_up: bfloat16 [3, 3, 512, 256], P(None, None, None, 'section'), may hold values from -0.09375 to 0.09375
- conv_second: bfloat16 [3, 3, 256, 256], P(None, None, None, 'section'), may hold values from -0.125 to 0.125
- conv_third_up: bfloat16 [3, 3, 256, 128], P(None, None, None, 'section'), may hold values from -0.125 to 0.125
- conv_third: bfloat16 [3, 3, 128, 128], P(None, None, None, 'section'), may hold values from -0.1875 to 0.1875
- conv_color: bfloat16 [3, 3, 128, 3], replicated, may hold values from -0.1875 to 0.1875
- gain_first: float32 [512], replicated, may hold values from 0.1 to 1.9
- gain_second: float32 [256], replicated, may hold values from 0.1 to 1.9
- gain_third: float32 [128], replicated, may hold values from 0.1 to 1.9
- gain_color: float32 [128], replicated, may hold values from 0.1 to 1.9
Outputs:
- handoff: float32 [2, 1024, 64], P('section', ('replica', 'seq')), parts along dimension 1
- image: float32 [3, 128, 512], P(None, ('replica', 'seq')), parts along dimension 1
The draws below stay inside these ranges and needn't reach their ends.
There are 2 independent parts, one for each index of `replica`. The reference program is written for one: setup_inputs(seed, part) draws one part's arguments, and reference() takes and returns one part's arrays. A program takes and returns all parts, laid end to end along the dimension named above; an argument that names none is the same for every part. Nothing has to cross between parts.
Inputs may be any that keep to these rules, and one draw needn't show every extreme that they name: `tile_start`: entry i is 1 where a decoder row tile begins at row block i; entry 0 is not read.
All inputs are finite; a program needn't handle non-finite values.
Results may differ from the reference program's by a relative error of at most 0.017.
Values may be sent and summed in bfloat16 or wider, within the bound.
A program may use at most 128 MiB of HBM per device.

```python
import math
import jax
import jax.numpy as jnp
from jax import lax

HEADS = 32
HSIZE = 128
HD = 4096
LCH = 16
PATCH = 64
TCOLS = 64
ROWS_DEV = 1
TOKENS = 512
SECTIONS = 2
AUDIO = 32
BLOCK = 16
BLOCKS = 32
TILES = 8
C1 = 512
C2 = 256
C3 = 128
RGB = 3
LROWS = 16
LCOLS = 128


def draw_cond(key, part):
    entries = jnp.clip(jax.random.normal(key, (SECTIONS, 3, TOKENS, HD), jnp.float32), -6.0, 6.0)
    return entries.astype(jnp.bfloat16)


def touch_ends(drawn, stream_key, low, top_value):
    longest = drawn.shape.index(max(drawn.shape))
    spots = []
    for shift in (0, 1):
        where = [jax.random.randint(jax.random.fold_in(stream_key, axis), (), 0, length) for axis, length in enumerate(drawn.shape)]
        where[longest] = (where[longest] + shift) % drawn.shape[longest]
        spots.append(tuple(where))
    return drawn.at[spots[0]].set(low).at[spots[1]].set(top_value)


def block_levels(own_key, shape, pieces, low, largest):
    loudness, own = 1.0, jax.random.fold_in(own_key, 6)
    for dim, shards_of in pieces:
        heights = jnp.exp(jax.random.uniform(jax.random.fold_in(own, dim), (shards_of,), jnp.float32, low / len(pieces), largest / len(pieces)))
        loudness = loudness * jnp.repeat(heights, shape[dim] // shards_of).reshape([-1 if axis == dim else 1 for axis in range(len(shape))])
    return loudness


def normal_values(rng, shape, scale, most, split=(), held_as=jnp.bfloat16):
    array = scale * jax.random.normal(rng, shape, jnp.float32)
    if split:
        array = array * block_levels(rng, shape, split, -0.22, 0.18)
    return jnp.clip(array, -most, most).astype(held_as)


def setup_inputs(seed: int = 0, part: int = 0) -> dict:
    arg_keys = jax.random.split(jax.random.key(seed), 19)
    part_keys = jax.random.split(jax.random.fold_in(arg_keys[18], part), 19)
    return {
        "latents": normal_values(part_keys[0], (SECTIONS, TOKENS, PATCH), 1.0, 6.0, ((0, 2), (1, 8)), jnp.float32),
        "cond": draw_cond(jax.random.fold_in(jax.random.fold_in(arg_keys[18], part), 71), part),
        "embed": normal_values(arg_keys[2], (SECTIONS, 3, PATCH, HD), PATCH ** -0.5, 0.75, ((0, 2),)),
        "audio_table": normal_values(part_keys[3], (SECTIONS, AUDIO, HD), 1.0, 6.0, ((0, 2),)),
        "audio_map": touch_ends(jax.random.randint(part_keys[4], (BLOCKS,), 0, AUDIO), jax.random.fold_in(part_keys[4], 1), 0, AUDIO - 1).astype(jnp.int32),
        "out_proj": normal_values(arg_keys[5], (SECTIONS, HD, PATCH), HSIZE ** -0.5, 0.5, ((0, 2),)),
        "tile_start": touch_ends((jax.random.randint(part_keys[6], (TILES,), 0, 4) < 1).astype(jnp.int32), jax.random.fold_in(part_keys[6], 1), 0, 1),
        "conv_input": normal_values(arg_keys[7], (3, 3, LCH, C1), (9 * LCH) ** -0.5, 0.5, ((3, 2),)),
        "conv_first": normal_values(arg_keys[8], (3, 3, C1, C1), (9 * C1) ** -0.5, 0.09375, ((3, 2),)),
        "conv_second_up": normal_values(arg_keys[9], (3, 3, C1, C2), (9 * C1) ** -0.5, 0.09375, ((3, 2),)),
        "conv_second": normal_values(arg_keys[10], (3, 3, C2, C2), (9 * C2) ** -0.5, 0.125, ((3, 2),)),
        "conv_third_up": normal_values(arg_keys[11], (3, 3, C2, C3), (9 * C2) ** -0.5, 0.125, ((3, 2),)),
        "conv_third": normal_values(arg_keys[12], (3, 3, C3, C3), (9 * C3) ** -0.5, 0.1875, ((3, 2),)),
        "conv_color": normal_values(arg_keys[13], (3, 3, C3, RGB), (9 * C3) ** -0.5, 0.1875),
        "gain_first": jnp.clip(1.0 + 0.18 * jax.random.normal(arg_keys[14], (C1,), jnp.float32), 0.1, 1.9),
        "gain_second": jnp.clip(1.0 + 0.18 * jax.random.normal(arg_keys[15], (C2,), jnp.float32), 0.1, 1.9),
        "gain_third": jnp.clip(1.0 + 0.18 * jax.random.normal(arg_keys[16], (C3,), jnp.float32), 0.1, 1.9),
        "gain_color": jnp.clip(1.0 + 0.18 * jax.random.normal(arg_keys[17], (C3,), jnp.float32), 0.1, 1.9),
    }


step_size = -0.5
norm_eps = 1e-06

def activate(field, gain):
    values = field.astype(jnp.float32)
    square_mean = lax.optimization_barrier(jnp.mean(values * values, axis=-1, keepdims=True))
    scaled = values * lax.rsqrt(square_mean + norm_eps) * gain
    return jax.nn.silu(scaled).astype(jnp.bfloat16)

def upsample(field):
    return jnp.repeat(jnp.repeat(field, 2, axis=0), 2, axis=1)

def tiled_conv(field, weight, tile_rows):
    height = field.shape[0]
    cols = field.shape[1]
    zero_row = jnp.zeros_like(field[:1])
    padded = jnp.concatenate([zero_row, field, zero_row], axis=0)
    zero_col = jnp.zeros_like(padded[:, :1])
    padded = jnp.concatenate([zero_col, padded, zero_col], axis=1)
    edge_tiles = jnp.concatenate([jnp.full((1,), -1, jnp.int32), tile_rows.astype(jnp.int32), jnp.full((1,), -2, jnp.int32)])
    result = jnp.zeros((height, cols, weight.shape[3]), jnp.float32)
    for row_tap in range(3):
        same_tile = (edge_tiles[row_tap:row_tap + height] == tile_rows).astype(field.dtype)
        for col_tap in range(3):
            window = padded[row_tap:row_tap + height, col_tap:col_tap + cols] * same_tile[:, None, None]
            product = jnp.dot(window.reshape(height * cols, -1), weight[row_tap, col_tap], preferred_element_type=jnp.float32)
            result = result + product.reshape(height, cols, -1)
    return result

def head_attention(trio):
    queries, key_rows, value_rows = trio
    scores = jnp.dot(queries, key_rows.T, preferred_element_type=jnp.float32) * (1.0 / math.sqrt(HSIZE))
    row_max = lax.optimization_barrier(jnp.max(scores, axis=1, keepdims=True))
    weights = jnp.exp(scores - row_max)
    denominator = lax.optimization_barrier(jnp.sum(weights, axis=1, keepdims=True))
    attended = jnp.dot(weights.astype(jnp.bfloat16), value_rows, preferred_element_type=jnp.float32) / denominator
    return attended.astype(jnp.bfloat16)

def split_heads(field):
    return field.reshape(TOKENS, HEADS, HSIZE).transpose(1, 0, 2)

def section_step(latent, cond_section, embed_section, table_section, frames, out_section):
    low = latent.astype(jnp.bfloat16)
    projected = jnp.einsum('tp,cph->cth', low.astype(jnp.float32), embed_section.astype(jnp.float32))
    audio = table_section[frames].astype(jnp.float32)
    queries = (projected[0] + cond_section[0].astype(jnp.float32) + audio).astype(jnp.bfloat16)
    key_rows = (projected[1] + cond_section[1].astype(jnp.float32)).astype(jnp.bfloat16)
    value_rows = (projected[2] + cond_section[2].astype(jnp.float32) + audio).astype(jnp.bfloat16)
    attended = lax.map(head_attention, (split_heads(queries), split_heads(key_rows), split_heads(value_rows)))
    mixed = attended.transpose(1, 0, 2).reshape(TOKENS, HEADS * HSIZE)
    velocity = jnp.dot(mixed, out_section, preferred_element_type=jnp.float32)
    return latent + step_size * velocity

def reference(latents, cond, embed, audio_table, audio_map, out_proj, tile_start, conv_input, conv_first, conv_second_up, conv_second, conv_third_up, conv_third, conv_color, gain_first, gain_second, gain_third, gain_color):
    frames = audio_map[jnp.arange(TOKENS, dtype=jnp.int32) // BLOCK]
    outcomes = []
    for section_index in range(SECTIONS):
        outcomes.append(section_step(latents[section_index], cond[section_index], embed[section_index], audio_table[section_index], frames, out_proj[section_index]))
    outcome = jnp.stack(outcomes)
    handoff = jnp.roll(outcome, 1, axis=0)
    final = outcome[SECTIONS - 1]
    grid = final.reshape(LROWS // 2, TCOLS, 2, 2, LCH).transpose(0, 2, 1, 3, 4).reshape(LROWS, LCOLS, LCH).astype(jnp.bfloat16)
    tiles = jnp.cumsum(tile_start).astype(jnp.int32)
    block_rows = 2 * ROWS_DEV
    tile_one = tiles[jnp.arange(LROWS, dtype=jnp.int32) // block_rows]
    tile_two = tiles[jnp.arange(2 * LROWS, dtype=jnp.int32) // (2 * block_rows)]
    tile_three = tiles[jnp.arange(4 * LROWS, dtype=jnp.int32) // (4 * block_rows)]
    first_a = tiled_conv(grid, conv_input, tile_one).astype(jnp.bfloat16)
    first_b = (first_a.astype(jnp.float32) + tiled_conv(activate(first_a, gain_first), conv_first, tile_one)).astype(jnp.bfloat16)
    second_a = tiled_conv(upsample(first_b), conv_second_up, tile_two).astype(jnp.bfloat16)
    second_b = (second_a.astype(jnp.float32) + tiled_conv(activate(second_a, gain_second), conv_second, tile_two)).astype(jnp.bfloat16)
    third_a = tiled_conv(upsample(second_b), conv_third_up, tile_three).astype(jnp.bfloat16)
    third_b = (third_a.astype(jnp.float32) + tiled_conv(activate(third_a, gain_third), conv_third, tile_three)).astype(jnp.bfloat16)
    colors = tiled_conv(activate(third_b, gain_color), conv_color, tile_three)
    return (handoff, colors.transpose(2, 0, 1))
```

```python
import math

import jax
import jax.numpy as jnp
from jax import lax
from jax.experimental import pallas as pl
from jax.experimental.pallas import tpu as pltpu
from jax.sharding import PartitionSpec as P

HEADS = 32
HSIZE = 128


step_size = -0.5
norm_eps = 1e-06


def full_weight(half):
    size = lax.axis_size("section")
    other = lax.ppermute(half, "section", [(i, (i + 1) % size) for i in range(size)])
    first = lax.axis_index("section") == 0
    return jnp.concatenate(
        [jnp.where(first, half, other), jnp.where(first, other, half)], axis=3
    )


def token_weight(weight):
    padded = jnp.pad(weight, ((2, 2), (2, 2), (0, 0), (0, 0)))
    cells = [[padded[1 - a : 7 - a, 1 - b : 7 - b] for b in (0, 1)] for a in (0, 1)]
    chans, outs = weight.shape[2:]
    stack = jnp.stack([jnp.stack(row) for row in cells])
    stack = stack.reshape(2, 2, 3, 2, 3, 2, chans, outs)
    return stack.transpose(2, 4, 3, 5, 6, 0, 1, 7).reshape(36 * chans, 4 * outs)


def lifted_weight(weight):
    wide = weight.astype(jnp.float32)
    taps = lambda w, axis: [
        [lax.index_in_dim(w, 0, axis, False),
         lax.index_in_dim(w, 1, axis, False) + lax.index_in_dim(w, 2, axis, False)],
        [lax.index_in_dim(w, 0, axis, False) + lax.index_in_dim(w, 1, axis, False),
         lax.index_in_dim(w, 2, axis, False)],
    ]
    rows = taps(wide, 0)
    cells = []
    for a in (0, 1):
        for b in (0, 1):
            parts = [taps(rows[a][p], 0)[b][q] for p in (0, 1) for q in (0, 1)]
            cells.append(jnp.concatenate(parts, axis=0).astype(jnp.bfloat16))
    return jnp.stack(cells)


def decode_kernel(
    keep, tokens, w_in, w_first, w_up2, w_second, w_up3, w_third, w_color,
    g1, g2, g3, g4, out, a1, p1, x1, a2, p2, x2, a3, p3, p4,
):
    cols = tokens.shape[1]
    f32, bf16 = jnp.float32, jnp.bfloat16
    k_a, k_b, k_c, k_d = keep[0], keep[1], keep[2], keep[3]

    def moved(value, by):
        position = lax.broadcasted_iota(jnp.int32, value.shape, 0)
        if by > 0:
            return jnp.where(position > 0, pltpu.roll(value, 1, 0), 0.0)
        return jnp.where(position < cols - 1, pltpu.roll(value, cols - 1, 0), 0.0)

    def put(buf, index, value):
        phases = value.shape[0]
        buf[index, 1 : phases + 1] = value.astype(bf16)
        buf[index, 0] = moved(value[phases - 1], 1).astype(bf16)
        buf[index, phases + 1] = moved(value[0], -1).astype(bf16)

    def act(value, gain):
        square = jnp.mean(value * value, axis=-1, keepdims=True)
        scaled = value * lax.rsqrt(square + norm_eps) * gain[...]
        return jax.nn.silu(scaled)

    def fill(source, buf, count, where_to, masked, gain=None, offset=0):
        @pl.loop(0, count)
        def _(i):
            value = source[i + offset].astype(f32)
            put(buf, where_to(i), value if gain is None else act(value, gain))

        for target, origin, factor in masked:
            if origin is None:
                buf[target] = jnp.zeros(buf.shape[1:], bf16)
            else:
                buf[target] = (buf[origin].astype(f32) * factor).astype(bf16)

    def spots(*bounds):
        def start(o):
            index = o
            for bound in bounds:
                index = index + 2 * (o >= bound).astype(jnp.int32)
            return index

        return start

    def window(buf, start, rows, taps_r, taps_c, phases):
        parts = []
        for p in taps_r:
            for q in taps_c:
                block = buf[pl.ds(start + p, rows), q : q + phases]
                parts.append(block.reshape(rows * phases * cols, block.shape[-1]))
        return jnp.concatenate(parts, axis=1)

    def dot(x, w):
        return jnp.dot(x, w, preferred_element_type=f32)

    full = tokens[...].astype(f32)
    count = full.shape[0]
    zero = jnp.zeros((1,) + full.shape[1:], f32)
    ks = (k_a, k_b, k_c, k_d)
    above = jnp.concatenate([zero] + [full[i : i + 1] * ks[i] for i in range(count - 1)])
    below = jnp.concatenate([full[i + 1 : i + 2] * ks[i] for i in range(count - 1)] + [zero])
    pieces = []
    for rows in (above, full, below):
        left = jnp.stack([moved(rows[i], 1) for i in range(count)])
        right = jnp.stack([moved(rows[i], -1) for i in range(count)])
        pieces += [left, rows, right]
    x = jnp.concatenate(pieces, axis=2).astype(bf16).reshape(count * cols, -1)
    c1 = a1.shape[-1]
    for a in (0, 1):
        for b in (0, 1):
            j = 2 * a + b
            y = dot(x, w_in[:, j * c1 : (j + 1) * c1]).astype(bf16)
            for i in range(count):
                a1[2 * i + a, b] = y[i * cols : (i + 1) * cols]

    def spot1(i):
        return i + 1 + 2 * (i >= 2).astype(jnp.int32) + 2 * (i >= 4).astype(jnp.int32)

    inner = ((3, 5, k_b), (4, 2, k_b), (7, 9, k_c), (8, 6, k_c))
    fill(a1, p1, 6, spot1, inner, g1, 2)
    for target, origin, factor in ((0, 1, k_a), (11, 8, k_d)):
        put(p1, target, act(a1[origin].astype(f32), g1) * factor)

    @pl.loop(0, 3)
    def _(i):
        y = dot(window(p1, 4 * i, 2, (0, 1, 2), (0, 1, 2), 2), w_first[...])
        base = a1[pl.ds(2 * i + 2, 2)]
        a1[pl.ds(2 * i + 2, 2)] = (base.astype(f32) + y.reshape(base.shape)).astype(bf16)

    fill(a1, x1, 6, spot1, inner + ((0, None, 0), (11, None, 0)), None, 2)

    @pl.loop(0, 3)
    def _(i):
        for a in (0, 1):
            for b in (0, 1):
                y = dot(window(x1, 4 * i, 2, (a, a + 1), (b, b + 1), 2), w_up2[2 * a + b])
                y = y.astype(bf16).reshape(2, 2, cols, -1)
                for r in (0, 1):
                    for f in (0, 1):
                        a2[4 * i + 2 * r + a, 2 * f + b] = y[r, f]

    fill(
        a2, p2, 10,
        lambda i: i + 2 * (i >= 3).astype(jnp.int32) + 2 * (i >= 7).astype(jnp.int32),
        ((3, 5, k_b), (4, 2, k_b), (9, 11, k_c), (10, 8, k_c)), g2, 1,
    )
    start2 = spots(2, 6)

    @pl.loop(0, 8)
    def _(o):
        y = dot(window(p2, start2(o), 1, (0, 1, 2), (0, 1, 2), 4), w_second[...])
        base = a2[o + 2]
        a2[o + 2] = (base.astype(f32) + y.reshape(base.shape)).astype(bf16)

    fill(
        a2, x2, 8,
        lambda i: i + 2 * (i >= 2).astype(jnp.int32) + 2 * (i >= 6).astype(jnp.int32),
        ((2, 4, k_b), (3, 1, k_b), (8, 10, k_c), (9, 7, k_c)), None, 2,
    )
    start3 = spots(1, 5)

    @pl.loop(0, 6)
    def _(o):
        for a in (0, 1):
            for b in (0, 1):
                y = dot(window(x2, start3(o), 1, (a, a + 1), (b, b + 1), 4), w_up3[2 * a + b])
                y = y.astype(bf16).reshape(4, cols, -1)
                for f in range(4):
                    a3[2 * o + a, 2 * f + b] = y[f]

    fill(
        a3, p3, 12,
        lambda i: i + 2 * (i >= 2).astype(jnp.int32) + 2 * (i >= 10).astype(jnp.int32),
        ((2, 4, k_b), (3, 1, k_b), (12, 14, k_c), (13, 11, k_c)), g3,
    )
    start4 = spots(1, 9)

    @pl.loop(0, 10)
    def _(o):
        y = dot(window(p3, start4(o), 1, (0, 1, 2), (0, 1, 2), 8), w_third[...])
        base = a3[o + 1]
        value = (base.astype(f32) + y.reshape(base.shape)).astype(bf16).astype(f32)
        put(p4, o, act(value, g4))

    for target, factor in ((0, k_b), (9, k_c)):
        p4[target] = (p4[target].astype(f32) * factor).astype(bf16)

    @pl.loop(0, 8)
    def _(o):
        patch = window(p4, o, 1, (0, 1, 2), (0, 1, 2), 8)
        out[o] = lax.dot_general(
            w_color[...], patch, (((1,), (1,)), ((), ())), preferred_element_type=f32
        )


def decode(tokens, keep, weights, gains):
    count, cols = tokens.shape[:2]
    c1, c2, c3 = (w.shape[-1] for w in (weights[1], weights[3], weights[5]))
    bf16 = jnp.bfloat16
    vmem = pl.BlockSpec(memory_space=pltpu.VMEM)
    rgb = weights[6].shape[0]
    return pl.pallas_call(
        decode_kernel,
        out_shape=jax.ShapeDtypeStruct((8, rgb, 8 * cols), jnp.float32),
        in_specs=[pl.BlockSpec(memory_space=pltpu.SMEM)] + [vmem] * 12,
        out_specs=vmem,
        scratch_shapes=[
            pltpu.VMEM((2 * count, 2, cols, c1), bf16),
            pltpu.VMEM((12, 4, cols, c1), bf16),
            pltpu.VMEM((12, 4, cols, c1), bf16),
            pltpu.VMEM((12, 4, cols, c2), bf16),
            pltpu.VMEM((14, 6, cols, c2), bf16),
            pltpu.VMEM((12, 6, cols, c2), bf16),
            pltpu.VMEM((12, 8, cols, c3), bf16),
            pltpu.VMEM((16, 10, cols, c3), bf16),
            pltpu.VMEM((10, 10, cols, c3), bf16),
        ],
        compiler_params=pltpu.CompilerParams(vmem_limit_bytes=56 * 1024 * 1024),
    )(keep, tokens, *weights, *gains)


def attend(queries, key_rows, value_rows, heads_here):
    query_count = queries.shape[0]
    head_width = queries.shape[1]
    head_size = head_width // heads_here
    scale = 1.0 / math.sqrt(head_size)
    key_heads = key_rows.reshape(-1, heads_here, head_size)
    value_heads = value_rows.reshape(-1, heads_here, head_size)
    query_block = min(512, query_count)
    blocks = queries.reshape(query_count // query_block, query_block, heads_here, head_size)

    def one_block(block_rows):
        scores = (
            jnp.einsum("qhd,khd->hqk", block_rows, key_heads, preferred_element_type=jnp.float32)
            * scale
        )
        row_max = jnp.max(scores, axis=2, keepdims=True)
        weights = jnp.exp(scores - row_max)
        denominator = jnp.sum(weights, axis=2, keepdims=True)
        attended = (
            jnp.einsum(
                "hqk,khd->hqd",
                weights.astype(jnp.bfloat16),
                value_heads,
                preferred_element_type=jnp.float32,
            )
            / denominator
        )
        return jnp.transpose(attended, (1, 0, 2)).astype(jnp.bfloat16)

    return lax.map(one_block, blocks).reshape(query_count, head_width)


def spread_full(projected_all, splits, groups, head_width):
    tokens_here = projected_all.shape[1]
    half_rows = tokens_here // splits
    devices = groups * splits
    pair_rows = projected_all[1:].reshape(2, tokens_here, groups, 1, head_width)
    pair_rows = jnp.broadcast_to(pair_rows, (2, tokens_here, groups, splits, head_width)).reshape(
        2, tokens_here, devices, head_width
    )
    query_rows = (
        projected_all[0]
        .reshape(splits, half_rows, groups, head_width)
        .transpose(1, 2, 0, 3)
        .reshape(1, half_rows, devices, head_width)
    )
    got_pairs, got_queries = (
        lax.all_to_all(pair_rows, "seq", split_axis=2, concat_axis=1, tiled=True),
        lax.all_to_all(query_rows, "seq", split_axis=2, concat_axis=1, tiled=True),
    )
    return (
        got_queries.reshape(-1, head_width),
        got_pairs[0].reshape(-1, head_width),
        got_pairs[1].reshape(-1, head_width),
    )


def body(
    latents,
    cond,
    embed,
    audio_table,
    audio_map,
    out_proj,
    tile_start,
    conv_input,
    conv_first,
    conv_second_up,
    conv_second,
    conv_third_up,
    conv_third,
    conv_color,
    gain_first,
    gain_second,
    gain_third,
    gain_color,
):
    split_convs = (conv_input, conv_first, conv_second_up, conv_second, conv_third_up, conv_third)
    latent = latents[0]
    tokens_here = latent.shape[0]
    low = latent.astype(jnp.bfloat16)
    projected = jnp.einsum("tp,cph->cth", low, embed[0], preferred_element_type=jnp.float32)
    frame_count = audio_table.shape[1]
    picks = (audio_map[:, None] == lax.broadcasted_iota(jnp.int32, (1, frame_count), 1)).astype(
        jnp.bfloat16
    )
    per_frame = jnp.dot(picks, audio_table[0], preferred_element_type=jnp.float32)
    audio = jnp.repeat(per_frame, tokens_here // audio_map.shape[0], axis=0)
    projected_all = jnp.stack(
        [
            (projected[0] + cond[0, 0] + audio).astype(jnp.bfloat16),
            (projected[1] + cond[0, 1]).astype(jnp.bfloat16),
            (projected[2] + cond[0, 2] + audio).astype(jnp.bfloat16),
        ]
    )
    devices = lax.axis_size("seq")
    splits = max(devices // HEADS, 1)
    per_device = max(HEADS // devices, 1)
    groups = HEADS // per_device
    head_width = per_device * HSIZE
    queries, key_rows, value_rows = spread_full(projected_all, splits, groups, head_width)
    attended = attend(queries, key_rows, value_rows, per_device)
    position = lax.axis_index("seq")
    group_rows = lax.dynamic_slice_in_dim(
        out_proj[0], (position // splits) * head_width, head_width, 0
    )
    partial = jnp.dot(attended, group_rows, preferred_element_type=jnp.float32)
    half_rows = tokens_here // splits
    partial = partial.reshape(devices, 1, half_rows, -1)
    if splits > 1:
        mine = lax.broadcasted_iota(jnp.int32, (1, splits, 1, 1), 1) == position % splits
        partial = jnp.where(mine, partial, 0.0)
    partial = partial.reshape(devices, tokens_here, -1)
    parts = lax.all_to_all(partial, "seq", split_axis=0, concat_axis=0, tiled=True)
    outcome = latent + step_size * jnp.sum(parts, axis=0)
    size = lax.axis_size("section")
    handed = lax.ppermute(outcome, "section", [(i, (i + 1) % size) for i in range(size)])
    final = jnp.where(lax.axis_index("section") == size - 1, outcome, handed)
    low_final = final.astype(jnp.bfloat16)
    rows = []
    for by in (-2, -1, 0, 1, 2):
        if by == 0:
            rows.append(low_final)
        else:
            pairs = [(i, i - by) for i in range(devices) if 0 <= i - by < devices]
            rows.append(lax.ppermute(low_final, "seq", pairs))
    tokens = jnp.stack(rows)
    block = position + jnp.arange(-2, 2)
    following = jnp.clip(block + 1, 0, devices - 1)
    inside = jnp.logical_and(block >= 0, block + 1 < devices)
    keep = jnp.where(jnp.logical_and(inside, tile_start[following] == 0), 1.0, 0.0)
    flat = lambda w: w.reshape(-1, w.shape[-1])
    w_input, w_first, w_up2, w_second, w_up3, w_third = [full_weight(w) for w in split_convs]
    color = jnp.pad(flat(conv_color).T, ((0, 8 - conv_color.shape[3]), (0, 0)))
    weights = (
        token_weight(w_input), flat(w_first), lifted_weight(w_up2), flat(w_second),
        lifted_weight(w_up3), flat(w_third), color,
    )
    gains = tuple(g[None] for g in (gain_first, gain_second, gain_third, gain_color))
    colors = decode(tokens, keep.astype(jnp.float32), weights, gains)
    rgb = conv_color.shape[3]
    image = colors[:, :rgb].reshape(8, rgb, 8, -1).transpose(1, 0, 3, 2).reshape(rgb, 8, -1)
    return (handed[None], image)


def solution(mesh):
    in_specs = (
        P("section", ("replica", "seq"), None),
        P("section", None, ("replica", "seq"), None),
        P("section", None, None, None),
        P("section", "replica", None),
        P(("replica", "seq")),
        P("section", None, None),
        P("replica"),
        P(None, None, None, "section"),
        P(None, None, None, "section"),
        P(None, None, None, "section"),
        P(None, None, None, "section"),
        P(None, None, None, "section"),
        P(None, None, None, "section"),
        P(),
        P(),
        P(),
        P(),
        P(),
    )
    out_specs = (P("section", ("replica", "seq"), None), P(None, ("replica", "seq"), None))
    return jax.shard_map(body, mesh=mesh, in_specs=in_specs, out_specs=out_specs, check_vma=False)
```

```python
import functools
import math

import jax
import jax.numpy as jnp
from jax import lax
from jax.experimental import pallas as pl
from jax.experimental.pallas import tpu as pltpu
from jax.sharding import PartitionSpec as P

HEADS = 32
HSIZE = 128


step_size = -0.5
norm_eps = 1e-06


MESH = pl.DeviceIdType.MESH


def lift(weight, lifted):
    depth = weight.shape[1]
    chunk = 64

    @pl.loop(0, depth // chunk)
    def _(i):
        row = pl.multiple_of(i * chunk, chunk)
        w = [weight[t, pl.ds(row, chunk)].astype(jnp.float32) for t in range(9)]

        def pairs(x, y, z):
            return ((x, y + z), (x + y, z))

        by_row = [pairs(w[q], w[3 + q], w[6 + q]) for q in range(3)]
        for a in (0, 1):
            for p in (0, 1):
                cols = pairs(*(by_row[q][a][p] for q in range(3)))
                for b in (0, 1):
                    for q in (0, 1):
                        at = pl.multiple_of((2 * p + q) * depth + row, chunk)
                        lifted[2 * a + b, pl.ds(at, chunk)] = cols[b][q].astype(jnp.bfloat16)


def front_kernel(
    splits, heads_here, sections, devices,
    latent, cond, embed, table, picks, out_proj, up2, up3, w_in, w_first, w_second, w_third,
    handed, tokens, o_up2, o_up3, i_up2, i_up3, i_in, i_first, i_second, i_third,
    proj, got_q, got_kv, partial, parts, result, low_final, rows, got_result, l_up2, l_up3,
    send_q, recv_q, send_kv, recv_kv, own_sem, send_p, recv_p, send_w, recv_w, keep_sem,
    send_h, recv_h, send_r, recv_r,
):
    f32, bf16 = jnp.float32, jnp.bfloat16
    me = lax.axis_index("seq")
    section = lax.axis_index("section")
    groups = devices // splits
    count = latent.shape[0]
    half = count // splits
    width = got_q.shape[1]
    size = width // heads_here
    my_group = me // splits

    barrier = pltpu.get_barrier_semaphore()
    for t in range(sections):

        @pl.loop(0, devices)
        def _(d):
            @pl.when(jnp.logical_or(d != me, section != t))
            def _():
                pl.semaphore_signal(
                    barrier, inc=1, device_id={"section": t, "seq": d}, device_id_type=MESH
                )

    pl.semaphore_wait(barrier, sections * devices - 1)

    low = latent[...].astype(bf16)
    partner = {"section": lax.rem(section + 1, sections)}

    def weight_copy(src, dst, k):
        return pltpu.make_async_remote_copy(
            src_ref=src, dst_ref=dst, send_sem=send_w.at[k], recv_sem=recv_w.at[k],
            device_id=partner, device_id_type=MESH,
        )

    def q_copy(d, src):
        return pltpu.make_async_remote_copy(
            src_ref=proj.at[d // splits, 0, pl.ds(lax.rem(d, splits) * half, half)],
            dst_ref=got_q.at[pl.ds(src * half, half)],
            send_sem=send_q.at[d], recv_sem=recv_q.at[src],
            device_id={"seq": d}, device_id_type=MESH,
        )

    def kv_copy(d, src):
        return pltpu.make_async_remote_copy(
            src_ref=proj.at[d // splits, pl.ds(1, 2)],
            dst_ref=got_kv.at[:, pl.ds(src * count, count)],
            send_sem=send_kv.at[d], recv_sem=recv_kv.at[src],
            device_id={"seq": d}, device_id_type=MESH,
        )

    @pl.loop(0, groups)
    def _(k):
        g = lax.rem(my_group + 1 + k, groups)
        lanes = pl.ds(pl.multiple_of(g * width, 128), width)
        audio = jnp.dot(picks[...], table[:, lanes], preferred_element_type=f32)
        for c in range(3):
            value = jnp.dot(low, embed[c, :, lanes], preferred_element_type=f32)
            value = value + cond[c, :, lanes].astype(f32)
            if c != 1:
                value = value + audio
            proj[g, c] = value.astype(bf16)

        @pl.loop(0, splits)
        def _(r):
            d = g * splits + r

            @pl.when(d != me)
            def _():
                q_copy(d, me).start()
                kv_copy(d, me).start()

    own_q = pltpu.make_async_copy(
        proj.at[my_group, 0, pl.ds(lax.rem(me, splits) * half, half)],
        got_q.at[pl.ds(me * half, half)], own_sem.at[0],
    )
    own_kv = pltpu.make_async_copy(
        proj.at[my_group, pl.ds(1, 2)], got_kv.at[:, pl.ds(me * count, count)], own_sem.at[1]
    )
    own_q.start()
    own_kv.start()
    plain = [
        weight_copy(w_in, i_in, 0), weight_copy(w_first, i_first, 1),
        weight_copy(w_second, i_second, 2), weight_copy(w_third, i_third, 3),
    ]
    for copy in plain:
        copy.start()
    lift(up2, l_up2)
    lift(up3, l_up3)
    made = [weight_copy(l_up2, i_up2, 4), weight_copy(l_up3, i_up3, 5)]
    kept = [
        pltpu.make_async_copy(l_up2, o_up2, keep_sem.at[0]),
        pltpu.make_async_copy(l_up3, o_up3, keep_sem.at[1]),
    ]
    for copy in made + kept:
        copy.start()

    own_q.wait()
    own_kv.wait()

    @pl.loop(0, devices)
    def _(d):
        @pl.when(d != me)
        def _():
            q_copy(d, d).wait_recv()
            kv_copy(d, d).wait_recv()

    query_count = got_q.shape[0]
    block = min(256, query_count)
    scale = 1.0 / math.sqrt(size)

    @pl.loop(0, query_count // block)
    def _(i):
        at = pl.ds(pl.multiple_of(i * block, block), block)
        total = jnp.zeros((block, out_proj.shape[1]), f32)
        for h in range(heads_here):
            lanes = slice(h * size, (h + 1) * size)
            scores = lax.dot_general(
                got_q[at, lanes], got_kv[0, :, lanes], (((1,), (1,)), ((), ())),
                preferred_element_type=f32,
            ) * scale
            row_max = jnp.max(scores, axis=1, keepdims=True)
            weights = jnp.exp(scores - row_max)
            denominator = jnp.sum(weights, axis=1, keepdims=True)
            attended = jnp.dot(
                weights.astype(bf16), got_kv[1, :, lanes], preferred_element_type=f32
            ) / denominator
            rows_of = pl.ds(pl.multiple_of(my_group * width + h * size, size), size)
            total = total + jnp.dot(
                attended.astype(bf16), out_proj[rows_of], preferred_element_type=f32
            )
        partial[at] = total

    def part_copy(d, src):
        return pltpu.make_async_remote_copy(
            src_ref=partial.at[pl.ds(d * half, half)],
            dst_ref=parts.at[src],
            send_sem=send_p.at[d], recv_sem=recv_p.at[src],
            device_id={"seq": d}, device_id_type=MESH,
        )

    @pl.loop(0, devices)
    def _(k):
        d = lax.rem(me + k, devices)

        @pl.when(d != me)
        def _():
            part_copy(d, me).start()

    @pl.loop(0, devices)
    def _(d):
        @pl.when(d != me)
        def _():
            part_copy(d, d).wait_recv()

    for r in range(splits):
        at = slice(r * half, (r + 1) * half)

        def add(g, total):
            d = g * splits + r
            own = partial[pl.ds(pl.multiple_of(me * half, half), half)]
            return total + jnp.where(d == me, own, parts[d])

        velocity = lax.fori_loop(0, groups, add, jnp.zeros((half, latent.shape[1]), f32))
        result[at] = latent[at] + step_size * velocity
    low_final[...] = result[...].astype(bf16)

    last = section == sections - 1
    given = pltpu.make_async_remote_copy(
        src_ref=result, dst_ref=got_result, send_sem=send_r, recv_sem=recv_r,
        device_id=partner, device_id_type=MESH,
    )
    given.start()

    def row_copy(by, t, to):
        slot = {2: 0, 1: 1, -1: 2, -2: 3}[by]
        return pltpu.make_async_remote_copy(
            src_ref=low_final, dst_ref=rows.at[slot],
            send_sem=send_h.at[slot, t], recv_sem=recv_h.at[slot],
            device_id={"section": t, "seq": lax.rem(to + devices, devices)}, device_id_type=MESH,
        )

    for by in (2, -2, 1, -1):
        for t in range(sections):
            inside = jnp.logical_and(me + by >= 0, me + by < devices)

            @pl.when(jnp.logical_and(last, inside))
            def _():
                row_copy(by, t, me + by).start()

    given.wait_recv()
    handed[...] = got_result[...]

    @pl.when(last)
    def _():
        tokens[2] = low_final[...]

    @pl.when(jnp.logical_not(last))
    def _():
        tokens[2] = got_result[...].astype(bf16)

    for by, slot, at in ((2, 0, 0), (1, 1, 1), (-1, 2, 3), (-2, 3, 4)):
        inside = jnp.logical_and(me - by >= 0, me - by < devices)

        @pl.when(inside)
        def _():
            row_copy(by, 0, me - by).wait_recv()
            tokens[at] = rows[slot]

        @pl.when(jnp.logical_not(inside))
        def _():
            tokens[at] = jnp.zeros(tokens.shape[1:], bf16)

    for by in (2, -2, 1, -1):
        for t in range(sections):
            inside = jnp.logical_and(me + by >= 0, me + by < devices)

            @pl.when(jnp.logical_and(last, inside))
            def _():
                row_copy(by, t, me + by).wait_send()

    given.wait_send()

    @pl.loop(0, devices)
    def _(d):
        @pl.when(d != me)
        def _():
            q_copy(d, me).wait_send()
            kv_copy(d, me).wait_send()
            part_copy(d, me).wait_send()

    for copy in kept + plain + made:
        copy.wait()


def front(latent, cond, embed, table, picks, out_proj, halves, splits, groups, width):
    w_in, w_first, up2, w_second, up3, w_third = halves
    devices, sections = lax.axis_size("seq"), lax.axis_size("section")
    f32, bf16 = jnp.float32, jnp.bfloat16
    count, patch = latent.shape
    half = count // splits
    heads_here = width // HSIZE
    vmem, hbm = pl.BlockSpec(memory_space=pltpu.VMEM), pl.BlockSpec(memory_space=pl.ANY)
    like = lambda a: jax.ShapeDtypeStruct(a.shape, a.dtype)
    lifted = lambda w: jax.ShapeDtypeStruct((4, 4 * w.shape[1], w.shape[2]), bf16)
    dma = pltpu.SemaphoreType.DMA
    l2, l3 = lifted(up2), lifted(up3)
    return pl.pallas_call(
        functools.partial(front_kernel, splits, heads_here, sections, devices),
        out_shape=(
            like(latent), jax.ShapeDtypeStruct((5, count, patch), bf16),
            l2, l3, l2, l3, like(w_in), like(w_first), like(w_second), like(w_third),
        ),
        in_specs=[vmem] * 8 + [hbm] * 4,
        out_specs=(vmem, vmem) + (hbm,) * 8,
        scratch_shapes=[
            pltpu.VMEM((groups, 3, count, width), bf16),
            pltpu.VMEM((devices * half, width), bf16),
            pltpu.VMEM((2, devices * count, width), bf16),
            pltpu.VMEM((devices * half, patch), f32),
            pltpu.VMEM((devices, half, patch), f32),
            pltpu.VMEM((count, patch), f32),
            pltpu.VMEM((count, patch), bf16),
            pltpu.VMEM((4, count, patch), bf16),
            pltpu.VMEM((count, patch), f32),
            pltpu.VMEM(l2.shape, bf16),
            pltpu.VMEM(l3.shape, bf16),
            dma((devices,)), dma((devices,)), dma((devices,)), dma((devices,)), dma((2,)),
            dma((devices,)), dma((devices,)), dma((6,)), dma((6,)), dma((2,)),
            dma((4, sections)), dma((4,)), dma, dma,
        ],
        compiler_params=pltpu.CompilerParams(
            collective_id=0, has_side_effects=True, vmem_limit_bytes=48 * 1024 * 1024
        ),
    )(latent, cond, embed, table, picks, out_proj, up2, up3, w_in, w_first, w_second, w_third)


def decode_kernel(
    keep, tokens, w_color, g1, g2, g3, g4,
    h_in, h_first, h_up2, h_second, h_up3, h_third,
    t_in, t_first, t_up2, t_second, t_up3, t_third,
    out, a1, p1, x1, a2, p2, x2, a3, p3, p4,
    w_in, w_first, w_up2, w_second, b_up3, b_third, w_up3, w_third, sems,
):
    section = lax.axis_index("section")
    loads = []
    for own, source in ((0, (h_in, h_first, h_up2, h_second, h_up3, h_third)),
                        (1, (t_in, t_first, t_up2, t_second, t_up3, t_third))):
        place = lax.rem(section + own, 2)
        for k, (src, dst) in enumerate(
            zip(source, (w_in, w_first, w_up2, w_second, b_up3, b_third))
        ):
            if k < 4:
                lanes = src.shape[-1]
                at = pl.ds(pl.multiple_of(place * lanes, 128), lanes)
                view = dst.at[:, :, at] if len(dst.shape) == 3 else dst.at[:, at]
            else:
                view = dst.at[place]
            copy = pltpu.make_async_copy(src, view, sems.at[own, k])
            copy.start()
            loads.append((k, copy))

    def ready(index):
        for k, copy in loads:
            if k == index:
                copy.wait()

    cols = tokens.shape[1]
    f32, bf16 = jnp.float32, jnp.bfloat16
    k_a, k_b, k_c, k_d = keep[0], keep[1], keep[2], keep[3]

    def moved(value, by):
        position = lax.broadcasted_iota(jnp.int32, value.shape, 0)
        if by > 0:
            return jnp.where(position > 0, pltpu.roll(value, 1, 0), 0.0)
        return jnp.where(position < cols - 1, pltpu.roll(value, cols - 1, 0), 0.0)

    def put(buf, index, value):
        phases = value.shape[0]
        buf[index, 1 : phases + 1] = value.astype(bf16)
        buf[index, 0] = moved(value[phases - 1], 1).astype(bf16)
        buf[index, phases + 1] = moved(value[0], -1).astype(bf16)

    def act(value, gain):
        square = jnp.mean(value * value, axis=-1, keepdims=True)
        scaled = value * lax.rsqrt(square + norm_eps) * gain[...]
        return jax.nn.silu(scaled)

    def fill(source, buf, count, where_to, masked, gain=None, offset=0):
        @pl.loop(0, count)
        def _(i):
            value = source[i + offset].astype(f32)
            put(buf, where_to(i), value if gain is None else act(value, gain))

        for target, origin, factor in masked:
            if origin is None:
                buf[target] = jnp.zeros(buf.shape[1:], bf16)
            else:
                buf[target] = (buf[origin].astype(f32) * factor).astype(bf16)

    def spots(*bounds):
        def start(o):
            index = o
            for bound in bounds:
                index = index + 2 * (o >= bound).astype(jnp.int32)
            return index

        return start

    def window(buf, start, rows, taps_r, taps_c, phases):
        parts = []
        for p in taps_r:
            for q in taps_c:
                block = buf[pl.ds(start + p, rows), q : q + phases]
                parts.append(block.reshape(rows * phases * cols, block.shape[-1]))
        return jnp.concatenate(parts, axis=1)

    def dot(x, w):
        return jnp.dot(x, w, preferred_element_type=f32)

    full = tokens[...].astype(f32)
    count = full.shape[0]
    zero = jnp.zeros((1,) + full.shape[1:], f32)
    ks = (k_a, k_b, k_c, k_d)
    above = jnp.concatenate([zero] + [full[i : i + 1] * ks[i] for i in range(count - 1)])
    below = jnp.concatenate([full[i + 1 : i + 2] * ks[i] for i in range(count - 1)] + [zero])
    pieces = []
    for rows in (above, full, below):
        left = jnp.stack([moved(rows[i], 1) for i in range(count)])
        right = jnp.stack([moved(rows[i], -1) for i in range(count)])
        pieces += [left, rows, right]
    x = jnp.concatenate(pieces, axis=2).astype(bf16).reshape(count * cols, -1)
    cell = tokens.shape[2]
    chans = cell // 4
    column = lax.broadcasted_iota(jnp.int32, (9 * cell, 9 * chans), 1)
    line = lax.broadcasted_iota(jnp.int32, (9 * cell, 9 * chans), 0)
    tap = column // chans
    tap_r = (tap >= 3).astype(jnp.int32) + (tap >= 6).astype(jnp.int32)
    tap_c = tap - 3 * tap_r
    ready(0)
    for a in (0, 1):
        for b in (0, 1):
            u, v = tap_r + (a + 1), tap_c + (b + 1)
            wanted = ((u >> 1) * 3 + (v >> 1)) * cell + (2 * (u & 1) + (v & 1)) * chans
            pick = (line == wanted + column - tap * chans).astype(f32).astype(bf16)
            y = dot(dot(x, pick).astype(bf16), w_in[...]).astype(bf16)
            for i in range(count):
                a1[2 * i + a, b] = y[i * cols : (i + 1) * cols]

    def spot1(i):
        return i + 1 + 2 * (i >= 2).astype(jnp.int32) + 2 * (i >= 4).astype(jnp.int32)

    inner = ((3, 5, k_b), (4, 2, k_b), (7, 9, k_c), (8, 6, k_c))
    fill(a1, p1, 6, spot1, inner, g1, 2)
    for target, origin, factor in ((0, 1, k_a), (11, 8, k_d)):
        put(p1, target, act(a1[origin].astype(f32), g1) * factor)
    ready(1)

    @pl.loop(0, 3)
    def _(i):
        y = dot(window(p1, 4 * i, 2, (0, 1, 2), (0, 1, 2), 2), w_first[...])
        base = a1[pl.ds(2 * i + 2, 2)]
        a1[pl.ds(2 * i + 2, 2)] = (base.astype(f32) + y.reshape(base.shape)).astype(bf16)

    fill(a1, x1, 6, spot1, inner + ((0, None, 0), (11, None, 0)), None, 2)

    ready(2)
    @pl.loop(0, 3)
    def _(i):
        for a in (0, 1):
            for b in (0, 1):
                y = dot(window(x1, 4 * i, 2, (a, a + 1), (b, b + 1), 2), w_up2[2 * a + b])
                y = y.astype(bf16).reshape(2, 2, cols, -1)
                for r in (0, 1):
                    for f in (0, 1):
                        a2[4 * i + 2 * r + a, 2 * f + b] = y[r, f]

    fill(
        a2, p2, 10,
        lambda i: i + 2 * (i >= 3).astype(jnp.int32) + 2 * (i >= 7).astype(jnp.int32),
        ((3, 5, k_b), (4, 2, k_b), (9, 11, k_c), (10, 8, k_c)), g2, 1,
    )
    start2 = spots(2, 6)
    ready(3)

    @pl.loop(0, 8)
    def _(o):
        y = dot(window(p2, start2(o), 1, (0, 1, 2), (0, 1, 2), 4), w_second[...])
        base = a2[o + 2]
        a2[o + 2] = (base.astype(f32) + y.reshape(base.shape)).astype(bf16)

    fill(
        a2, x2, 8,
        lambda i: i + 2 * (i >= 2).astype(jnp.int32) + 2 * (i >= 6).astype(jnp.int32),
        ((2, 4, k_b), (3, 1, k_b), (8, 10, k_c), (9, 7, k_c)), None, 2,
    )
    start3 = spots(1, 5)

    ready(4)
    ready(5)
    w_up3[...] = jnp.concatenate([b_up3[0], b_up3[1]], axis=2)
    w_third[...] = jnp.concatenate([b_third[0], b_third[1]], axis=1)

    @pl.loop(0, 6)
    def _(o):
        for a in (0, 1):
            for b in (0, 1):
                y = dot(window(x2, start3(o), 1, (a, a + 1), (b, b + 1), 4), w_up3[2 * a + b])
                y = y.astype(bf16).reshape(4, cols, -1)
                for f in range(4):
                    a3[2 * o + a, 2 * f + b] = y[f]

    fill(
        a3, p3, 12,
        lambda i: i + 2 * (i >= 2).astype(jnp.int32) + 2 * (i >= 10).astype(jnp.int32),
        ((2, 4, k_b), (3, 1, k_b), (12, 14, k_c), (13, 11, k_c)), g3,
    )
    start4 = spots(1, 9)

    @pl.loop(0, 10)
    def _(o):
        y = dot(window(p3, start4(o), 1, (0, 1, 2), (0, 1, 2), 8), w_third[...])
        base = a3[o + 1]
        value = (base.astype(f32) + y.reshape(base.shape)).astype(bf16).astype(f32)
        put(p4, o, act(value, g4))

    for target, factor in ((0, k_b), (9, k_c)):
        p4[target] = (p4[target].astype(f32) * factor).astype(bf16)

    @pl.loop(0, 8)
    def _(o):
        patch = window(p4, o, 1, (0, 1, 2), (0, 1, 2), 8)
        colors = lax.dot_general(
            w_color[...], patch, (((1,), (1,)), ((), ())), preferred_element_type=f32
        )
        for k in range(out.shape[0]):
            out[k, pl.ds(o, 1)] = colors[k : k + 1]


def decode(tokens, keep, color, gains, own, other, rgb):
    count, cols = tokens.shape[:2]
    c1, c2, c3 = (2 * own[k].shape[-1] for k in (1, 3, 5))
    bf16 = jnp.bfloat16
    vmem, hbm = pl.BlockSpec(memory_space=pltpu.VMEM), pl.BlockSpec(memory_space=pl.ANY)
    wide = lambda w: pltpu.VMEM(w.shape[:-1] + (2 * w.shape[-1],), bf16)
    return pl.pallas_call(
        decode_kernel,
        out_shape=jax.ShapeDtypeStruct((rgb, 8, 8 * cols), jnp.float32),
        in_specs=[pl.BlockSpec(memory_space=pltpu.SMEM)] + [vmem] * 6 + [hbm] * 12,
        out_specs=vmem,
        scratch_shapes=[
            pltpu.VMEM((2 * count, 2, cols, c1), bf16),
            pltpu.VMEM((12, 4, cols, c1), bf16),
            pltpu.VMEM((12, 4, cols, c1), bf16),
            pltpu.VMEM((12, 4, cols, c2), bf16),
            pltpu.VMEM((14, 6, cols, c2), bf16),
            pltpu.VMEM((12, 6, cols, c2), bf16),
            pltpu.VMEM((12, 8, cols, c3), bf16),
            pltpu.VMEM((16, 10, cols, c3), bf16),
            pltpu.VMEM((10, 10, cols, c3), bf16),
            wide(own[0]), wide(own[1]), wide(own[2]), wide(own[3]),
            pltpu.VMEM((2,) + own[4].shape, bf16), pltpu.VMEM((2,) + own[5].shape, bf16),
            wide(own[4]), wide(own[5]),
            pltpu.SemaphoreType.DMA((2, 6)),
        ],
        compiler_params=pltpu.CompilerParams(vmem_limit_bytes=56 * 1024 * 1024),
    )(keep, tokens, color, *gains, *own, *other)


def body(
    latents,
    cond,
    embed,
    audio_table,
    audio_map,
    out_proj,
    tile_start,
    conv_input,
    conv_first,
    conv_second_up,
    conv_second,
    conv_third_up,
    conv_third,
    conv_color,
    gain_first,
    gain_second,
    gain_third,
    gain_color,
):
    latent = latents[0]
    tokens_here = latent.shape[0]
    frame_count = audio_table.shape[1]
    frames = jnp.repeat(audio_map, tokens_here // audio_map.shape[0])
    picks = (frames[:, None] == lax.broadcasted_iota(jnp.int32, (1, frame_count), 1)).astype(
        jnp.bfloat16
    )
    devices = lax.axis_size("seq")
    splits = max(devices // HEADS, 1)
    per_device = max(HEADS // devices, 1)
    groups = HEADS // per_device
    flat = lambda w: w.reshape(-1, w.shape[-1])
    taps = lambda w: w.reshape(9, *w.shape[2:])
    halves = (
        flat(conv_input), flat(conv_first), taps(conv_second_up),
        flat(conv_second), taps(conv_third_up), flat(conv_third),
    )
    handed, tokens, o_up2, o_up3, i_up2, i_up3, i_in, i_first, i_second, i_third = front(
        latent, cond[0], embed[0], audio_table[0], picks, out_proj[0], halves, splits, groups,
        per_device * HSIZE,
    )
    position = lax.axis_index("seq")
    block = position + jnp.arange(-2, 2)
    following = jnp.clip(block + 1, 0, devices - 1)
    inside = jnp.logical_and(block >= 0, block + 1 < devices)
    keep = jnp.where(jnp.logical_and(inside, tile_start[following] == 0), 1.0, 0.0)
    color = jnp.pad(flat(conv_color).T, ((0, 8 - conv_color.shape[3]), (0, 0)))
    gains = tuple(g[None] for g in (gain_first, gain_second, gain_third, gain_color))
    own = (halves[0], halves[1], o_up2, halves[3], o_up3, halves[5])
    other = (i_in, i_first, i_up2, i_second, i_up3, i_third)
    rgb = conv_color.shape[3]
    colors = decode(tokens, keep.astype(jnp.float32), color, gains, own, other, rgb)
    image = colors.reshape(rgb, 8, 8, -1).transpose(0, 1, 3, 2).reshape(rgb, 8, -1)
    return (handed[None], image)


def solution(mesh):
    in_specs = (
        P("section", ("replica", "seq"), None),
        P("section", None, ("replica", "seq"), None),
        P("section", None, None, None),
        P("section", "replica", None),
        P(("replica", "seq")),
        P("section", None, None),
        P("replica"),
        P(None, None, None, "section"),
        P(None, None, None, "section"),
        P(None, None, None, "section"),
        P(None, None, None, "section"),
        P(None, None, None, "section"),
        P(None, None, None, "section"),
        P(),
        P(),
        P(),
        P(),
        P(),
    )
    out_specs = (P("section", ("replica", "seq"), None), P(None, ("replica", "seq"), None))
    return jax.shard_map(body, mesh=mesh, in_specs=in_specs, out_specs=out_specs, check_vma=False)
```

```python
import functools
import math

import jax
import jax.numpy as jnp
from jax import lax
from jax.experimental import pallas as pl
from jax.experimental.pallas import tpu as pltpu
from jax.sharding import PartitionSpec as P

HEADS = 32
HSIZE = 128


step_size = -0.5
norm_eps = 1e-06


MESH = pl.DeviceIdType.MESH


def lift(weight, lifted):
    depth = weight.shape[1]
    chunk = 64

    @pl.loop(0, depth // chunk)
    def _(i):
        row = pl.multiple_of(i * chunk, chunk)
        w = [weight[t, pl.ds(row, chunk)].astype(jnp.float32) for t in range(9)]

        def pairs(x, y, z):
            return ((x, y + z), (x + y, z))

        by_row = [pairs(w[q], w[3 + q], w[6 + q]) for q in range(3)]
        for a in (0, 1):
            for p in (0, 1):
                cols = pairs(*(by_row[q][a][p] for q in range(3)))
                for b in (0, 1):
                    for q in (0, 1):
                        at = pl.multiple_of((2 * p + q) * depth + row, chunk)
                        lifted[2 * a + b, pl.ds(at, chunk)] = cols[b][q].astype(jnp.bfloat16)


def front_kernel(
    splits, heads_here, sections, devices,
    latent, cond, embed, table, picks, out_proj, up2, up3, w_in, w_first, w_second, w_third,
    handed, tokens, o_up2, o_up3, i_up2, i_up3, i_in, i_first, i_second, i_third,
    proj, got_q, got_kv, partial, parts, result, low_final, rows, got_result, l_up2, l_up3,
    send_q, recv_q, send_kv, recv_kv, own_sem, send_p, recv_p, send_w, recv_w, keep_sem,
    send_h, recv_h, send_r, recv_r,
):
    f32, bf16 = jnp.float32, jnp.bfloat16
    me = lax.axis_index("seq")
    section = lax.axis_index("section")
    groups = devices // splits
    count = latent.shape[0]
    half = count // splits
    width = got_q.shape[1]
    size = width // heads_here
    my_group = me // splits

    barrier = pltpu.get_barrier_semaphore()
    for t in range(sections):

        @pl.loop(0, devices)
        def _(d):
            @pl.when(jnp.logical_or(d != me, section != t))
            def _():
                pl.semaphore_signal(
                    barrier, inc=1, device_id={"section": t, "seq": d}, device_id_type=MESH
                )

    pl.semaphore_wait(barrier, sections * devices - 1)

    low = latent[...].astype(bf16)
    partner = {"section": lax.rem(section + 1, sections)}

    def weight_copy(src, dst, k):
        return pltpu.make_async_remote_copy(
            src_ref=src, dst_ref=dst, send_sem=send_w.at[k], recv_sem=recv_w.at[k],
            device_id=partner, device_id_type=MESH,
        )

    def q_copy(d, src):
        return pltpu.make_async_remote_copy(
            src_ref=proj.at[d // splits, 0, pl.ds(lax.rem(d, splits) * half, half)],
            dst_ref=got_q.at[pl.ds(src * half, half)],
            send_sem=send_q.at[d], recv_sem=recv_q.at[src],
            device_id={"seq": d}, device_id_type=MESH,
        )

    def kv_copy(d, src):
        return pltpu.make_async_remote_copy(
            src_ref=proj.at[d // splits, pl.ds(1, 2)],
            dst_ref=got_kv.at[:, pl.ds(src * count, count)],
            send_sem=send_kv.at[d], recv_sem=recv_kv.at[src],
            device_id={"seq": d}, device_id_type=MESH,
        )

    @pl.loop(0, groups)
    def _(k):
        g = lax.rem(my_group + 1 + k, groups)
        lanes = pl.ds(pl.multiple_of(g * width, 128), width)
        audio = jnp.dot(picks[...], table[:, lanes], preferred_element_type=f32)
        for c in range(3):
            value = jnp.dot(low, embed[c, :, lanes], preferred_element_type=f32)
            value = value + cond[c, :, lanes].astype(f32)
            if c != 1:
                value = value + audio
            proj[g, c] = value.astype(bf16)

        @pl.loop(0, splits)
        def _(r):
            d = g * splits + r

            @pl.when(d != me)
            def _():
                q_copy(d, me).start()
                kv_copy(d, me).start()

    own_q = pltpu.make_async_copy(
        proj.at[my_group, 0, pl.ds(lax.rem(me, splits) * half, half)],
        got_q.at[pl.ds(me * half, half)], own_sem.at[0],
    )
    own_kv = pltpu.make_async_copy(
        proj.at[my_group, pl.ds(1, 2)], got_kv.at[:, pl.ds(me * count, count)], own_sem.at[1]
    )
    own_q.start()
    own_kv.start()
    plain = [
        weight_copy(w_in, i_in, 0), weight_copy(w_first, i_first, 1),
        weight_copy(w_second, i_second, 2), weight_copy(w_third, i_third, 3),
    ]
    for copy in plain:
        copy.start()
    lift(up2, l_up2)
    lift(up3, l_up3)
    made = [weight_copy(l_up2, i_up2, 4), weight_copy(l_up3, i_up3, 5)]
    kept = [
        pltpu.make_async_copy(l_up2, o_up2, keep_sem.at[0]),
        pltpu.make_async_copy(l_up3, o_up3, keep_sem.at[1]),
    ]
    for copy in made + kept:
        copy.start()

    own_q.wait()
    own_kv.wait()

    @pl.loop(0, devices)
    def _(d):
        @pl.when(d != me)
        def _():
            q_copy(d, d).wait_recv()
            kv_copy(d, d).wait_recv()

    query_count = got_q.shape[0]
    block = min(256, query_count)
    scale = 1.0 / math.sqrt(size)

    @pl.loop(0, query_count // block)
    def _(i):
        at = pl.ds(pl.multiple_of(i * block, block), block)
        total = jnp.zeros((block, out_proj.shape[1]), f32)
        for h in range(heads_here):
            lanes = slice(h * size, (h + 1) * size)
            scores = lax.dot_general(
                got_q[at, lanes], got_kv[0, :, lanes], (((1,), (1,)), ((), ())),
                preferred_element_type=f32,
            ) * scale
            row_max = jnp.max(scores, axis=1, keepdims=True)
            weights = jnp.exp(scores - row_max)
            denominator = jnp.sum(weights, axis=1, keepdims=True)
            attended = jnp.dot(
                weights.astype(bf16), got_kv[1, :, lanes], preferred_element_type=f32
            ) / denominator
            rows_of = pl.ds(pl.multiple_of(my_group * width + h * size, size), size)
            total = total + jnp.dot(
                attended.astype(bf16), out_proj[rows_of], preferred_element_type=f32
            )
        partial[at] = total

    def part_copy(d, src):
        return pltpu.make_async_remote_copy(
            src_ref=partial.at[pl.ds(d * half, half)],
            dst_ref=parts.at[src],
            send_sem=send_p.at[d], recv_sem=recv_p.at[src],
            device_id={"seq": d}, device_id_type=MESH,
        )

    @pl.loop(0, devices)
    def _(k):
        d = lax.rem(me + k, devices)

        @pl.when(d != me)
        def _():
            part_copy(d, me).start()

    @pl.loop(0, devices)
    def _(d):
        @pl.when(d != me)
        def _():
            part_copy(d, d).wait_recv()

    for r in range(splits):
        at = slice(r * half, (r + 1) * half)

        def add(g, total):
            d = g * splits + r
            own = partial[pl.ds(pl.multiple_of(me * half, half), half)]
            return total + jnp.where(d == me, own, parts[d])

        velocity = lax.fori_loop(0, groups, add, jnp.zeros((half, latent.shape[1]), f32))
        result[at] = latent[at] + step_size * velocity
    low_final[...] = result[...].astype(bf16)

    last = section == sections - 1
    given = pltpu.make_async_remote_copy(
        src_ref=result, dst_ref=got_result, send_sem=send_r, recv_sem=recv_r,
        device_id=partner, device_id_type=MESH,
    )
    given.start()

    def row_copy(by, t, to):
        slot = {2: 0, 1: 1, -1: 2, -2: 3}[by]
        return pltpu.make_async_remote_copy(
            src_ref=low_final, dst_ref=rows.at[slot],
            send_sem=send_h.at[slot, t], recv_sem=recv_h.at[slot],
            device_id={"section": t, "seq": lax.rem(to + devices, devices)}, device_id_type=MESH,
        )

    for by in (2, -2, 1, -1):
        for t in range(sections):
            inside = jnp.logical_and(me + by >= 0, me + by < devices)

            @pl.when(jnp.logical_and(last, inside))
            def _():
                row_copy(by, t, me + by).start()

    given.wait_recv()
    handed[...] = got_result[...]

    @pl.when(last)
    def _():
        tokens[2] = low_final[...]

    @pl.when(jnp.logical_not(last))
    def _():
        tokens[2] = got_result[...].astype(bf16)

    for by, slot, at in ((2, 0, 0), (1, 1, 1), (-1, 2, 3), (-2, 3, 4)):
        inside = jnp.logical_and(me - by >= 0, me - by < devices)

        @pl.when(inside)
        def _():
            row_copy(by, 0, me - by).wait_recv()
            tokens[at] = rows[slot]

        @pl.when(jnp.logical_not(inside))
        def _():
            tokens[at] = jnp.zeros(tokens.shape[1:], bf16)

    for by in (2, -2, 1, -1):
        for t in range(sections):
            inside = jnp.logical_and(me + by >= 0, me + by < devices)

            @pl.when(jnp.logical_and(last, inside))
            def _():
                row_copy(by, t, me + by).wait_send()

    given.wait_send()

    @pl.loop(0, devices)
    def _(d):
        @pl.when(d != me)
        def _():
            q_copy(d, me).wait_send()
            kv_copy(d, me).wait_send()
            part_copy(d, me).wait_send()

    for copy in kept + plain + made:
        copy.wait()


def front(latent, cond, embed, table, picks, out_proj, halves, splits, groups, width):
    w_in, w_first, up2, w_second, up3, w_third = halves
    devices, sections = lax.axis_size("seq"), lax.axis_size("section")
    f32, bf16 = jnp.float32, jnp.bfloat16
    count, patch = latent.shape
    half = count // splits
    heads_here = width // HSIZE
    vmem, hbm = pl.BlockSpec(memory_space=pltpu.VMEM), pl.BlockSpec(memory_space=pl.ANY)
    like = lambda a: jax.ShapeDtypeStruct(a.shape, a.dtype)
    lifted = lambda w: jax.ShapeDtypeStruct((4, 4 * w.shape[1], w.shape[2]), bf16)
    dma = pltpu.SemaphoreType.DMA
    l2, l3 = lifted(up2), lifted(up3)
    return pl.pallas_call(
        functools.partial(front_kernel, splits, heads_here, sections, devices),
        out_shape=(
            like(latent), jax.ShapeDtypeStruct((5, count, patch), bf16),
            l2, l3, l2, l3, like(w_in), like(w_first), like(w_second), like(w_third),
        ),
        in_specs=[vmem] * 8 + [hbm] * 4,
        out_specs=(vmem, vmem) + (hbm,) * 8,
        scratch_shapes=[
            pltpu.VMEM((groups, 3, count, width), bf16),
            pltpu.VMEM((devices * half, width), bf16),
            pltpu.VMEM((2, devices * count, width), bf16),
            pltpu.VMEM((devices * half, patch), f32),
            pltpu.VMEM((devices, half, patch), f32),
            pltpu.VMEM((count, patch), f32),
            pltpu.VMEM((count, patch), bf16),
            pltpu.VMEM((4, count, patch), bf16),
            pltpu.VMEM((count, patch), f32),
            pltpu.VMEM(l2.shape, bf16),
            pltpu.VMEM(l3.shape, bf16),
            dma((devices,)), dma((devices,)), dma((devices,)), dma((devices,)), dma((2,)),
            dma((devices,)), dma((devices,)), dma((6,)), dma((6,)), dma((2,)),
            dma((4, sections)), dma((4,)), dma, dma,
        ],
        compiler_params=pltpu.CompilerParams(
            collective_id=0, has_side_effects=True, vmem_limit_bytes=48 * 1024 * 1024
        ),
    )(latent, cond, embed, table, picks, out_proj, up2, up3, w_in, w_first, w_second, w_third)


def decode_kernel(
    keep, tokens, w_color, g1, g2, g3, g4,
    h_in, h_first, h_up2, h_second, h_up3, h_third,
    t_in, t_first, t_up2, t_second, t_up3, t_third,
    out, a1, p1, x1, a2, p2, x2, a3, p3, p4,
    w_in, w_first, w_up2, w_second, b_up3, b_third, w_up3, w_third, sems,
):
    section = lax.axis_index("section")
    loads = []
    for own, source in ((0, (h_in, h_first, h_up2, h_second, h_up3, h_third)),
                        (1, (t_in, t_first, t_up2, t_second, t_up3, t_third))):
        place = lax.rem(section + own, 2)
        for k, (src, dst) in enumerate(
            zip(source, (w_in, w_first, w_up2, w_second, b_up3, b_third))
        ):
            if k < 4:
                lanes = src.shape[-1]
                at = pl.ds(pl.multiple_of(place * lanes, 128), lanes)
                view = dst.at[:, :, at] if len(dst.shape) == 3 else dst.at[:, at]
            else:
                view = dst.at[place]
            copy = pltpu.make_async_copy(src, view, sems.at[own, k])
            copy.start()
            loads.append((k, copy))

    def ready(index):
        for k, copy in loads:
            if k == index:
                copy.wait()

    cols = tokens.shape[1]
    f32, bf16 = jnp.float32, jnp.bfloat16
    k_a, k_b, k_c, k_d = keep[0], keep[1], keep[2], keep[3]

    def moved(value, by):
        position = lax.broadcasted_iota(jnp.int32, value.shape, 0)
        if by > 0:
            return jnp.where(position > 0, pltpu.roll(value, 1, 0), 0.0)
        return jnp.where(position < cols - 1, pltpu.roll(value, cols - 1, 0), 0.0)

    def put(buf, index, value):
        phases = value.shape[0]
        buf[index, 1 : phases + 1] = value.astype(bf16)
        buf[index, 0] = moved(value[phases - 1], 1).astype(bf16)
        buf[index, phases + 1] = moved(value[0], -1).astype(bf16)

    def act(value, gain):
        square = jnp.mean(value * value, axis=-1, keepdims=True)
        scaled = value * lax.rsqrt(square + norm_eps) * gain[...]
        return jax.nn.silu(scaled)

    def fill(source, buf, count, where_to, masked, gain=None, offset=0):
        @pl.loop(0, count)
        def _(i):
            value = source[i + offset].astype(f32)
            put(buf, where_to(i), value if gain is None else act(value, gain))

        for target, origin, factor in masked:
            if origin is None:
                buf[target] = jnp.zeros(buf.shape[1:], bf16)
            else:
                buf[target] = (buf[origin].astype(f32) * factor).astype(bf16)

    def spots(*bounds):
        def start(o):
            index = o
            for bound in bounds:
                index = index + 2 * (o >= bound).astype(jnp.int32)
            return index

        return start

    def window(buf, start, rows, taps_r, taps_c, phases):
        parts = []
        for p in taps_r:
            for q in taps_c:
                block = buf[pl.ds(start + p, rows), q : q + phases]
                parts.append(block.reshape(rows * phases * cols, block.shape[-1]))
        return jnp.concatenate(parts, axis=1)

    def dot(x, w):
        return jnp.dot(x, w, preferred_element_type=f32)

    full = tokens[...].astype(f32)
    count = full.shape[0]
    zero = jnp.zeros((1,) + full.shape[1:], f32)
    ks = (k_a, k_b, k_c, k_d)
    above = jnp.concatenate([zero] + [full[i : i + 1] * ks[i] for i in range(count - 1)])
    below = jnp.concatenate([full[i + 1 : i + 2] * ks[i] for i in range(count - 1)] + [zero])
    pieces = []
    for rows in (above, full, below):
        left = jnp.stack([moved(rows[i], 1) for i in range(count)])
        right = jnp.stack([moved(rows[i], -1) for i in range(count)])
        pieces += [left, rows, right]
    x = jnp.concatenate(pieces, axis=2).astype(bf16).reshape(count * cols, -1)
    cell = tokens.shape[2]
    chans = cell // 4
    column = lax.broadcasted_iota(jnp.int32, (9 * cell, 9 * chans), 1)
    line = lax.broadcasted_iota(jnp.int32, (9 * cell, 9 * chans), 0)
    tap = column // chans
    tap_r = (tap >= 3).astype(jnp.int32) + (tap >= 6).astype(jnp.int32)
    tap_c = tap - 3 * tap_r
    ready(0)
    for a in (0, 1):
        for b in (0, 1):
            u, v = tap_r + (a + 1), tap_c + (b + 1)
            wanted = ((u >> 1) * 3 + (v >> 1)) * cell + (2 * (u & 1) + (v & 1)) * chans
            pick = (line == wanted + column - tap * chans).astype(f32).astype(bf16)
            y = dot(dot(x, pick).astype(bf16), w_in[...]).astype(bf16)
            for i in range(count):
                a1[2 * i + a, b] = y[i * cols : (i + 1) * cols]

    def spot1(i):
        return i + 1 + 2 * (i >= 2).astype(jnp.int32) + 2 * (i >= 4).astype(jnp.int32)

    inner = ((3, 5, k_b), (4, 2, k_b), (7, 9, k_c), (8, 6, k_c))
    fill(a1, p1, 6, spot1, inner, g1, 2)
    for target, origin, factor in ((0, 1, k_a), (11, 8, k_d)):
        put(p1, target, act(a1[origin].astype(f32), g1) * factor)
    ready(1)

    @pl.loop(0, 3)
    def _(i):
        y = dot(window(p1, 4 * i, 2, (0, 1, 2), (0, 1, 2), 2), w_first[...])
        base = a1[pl.ds(2 * i + 2, 2)]
        a1[pl.ds(2 * i + 2, 2)] = (base.astype(f32) + y.reshape(base.shape)).astype(bf16)

    fill(a1, x1, 6, spot1, inner + ((0, None, 0), (11, None, 0)), None, 2)

    ready(2)
    @pl.loop(0, 3)
    def _(i):
        for a in (0, 1):
            for b in (0, 1):
                y = dot(window(x1, 4 * i, 2, (a, a + 1), (b, b + 1), 2), w_up2[2 * a + b])
                y = y.astype(bf16).reshape(2, 2, cols, -1)
                for r in (0, 1):
                    for f in (0, 1):
                        a2[4 * i + 2 * r + a, 2 * f + b] = y[r, f]

    fill(
        a2, p2, 10,
        lambda i: i + 2 * (i >= 3).astype(jnp.int32) + 2 * (i >= 7).astype(jnp.int32),
        ((3, 5, k_b), (4, 2, k_b), (9, 11, k_c), (10, 8, k_c)), g2, 1,
    )
    start2 = spots(2, 6)
    ready(3)

    @pl.loop(0, 8)
    def _(o):
        y = dot(window(p2, start2(o), 1, (0, 1, 2), (0, 1, 2), 4), w_second[...])
        base = a2[o + 2]
        a2[o + 2] = (base.astype(f32) + y.reshape(base.shape)).astype(bf16)

    fill(
        a2, x2, 8,
        lambda i: i + 2 * (i >= 2).astype(jnp.int32) + 2 * (i >= 6).astype(jnp.int32),
        ((2, 4, k_b), (3, 1, k_b), (8, 10, k_c), (9, 7, k_c)), None, 2,
    )
    start3 = spots(1, 5)

    ready(4)
    ready(5)
    w_up3[...] = jnp.concatenate([b_up3[0], b_up3[1]], axis=2)
    w_third[...] = jnp.concatenate([b_third[0], b_third[1]], axis=1)

    @pl.loop(0, 6)
    def _(o):
        for a in (0, 1):
            for b in (0, 1):
                y = dot(window(x2, start3(o), 1, (a, a + 1), (b, b + 1), 4), w_up3[2 * a + b])
                y = y.astype(bf16).reshape(4, cols, -1)
                for f in range(4):
                    a3[2 * o + a, 2 * f + b] = y[f]

    fill(
        a3, p3, 12,
        lambda i: i + 2 * (i >= 2).astype(jnp.int32) + 2 * (i >= 10).astype(jnp.int32),
        ((2, 4, k_b), (3, 1, k_b), (12, 14, k_c), (13, 11, k_c)), g3,
    )
    start4 = spots(1, 9)

    @pl.loop(0, 10)
    def _(o):
        y = dot(window(p3, start4(o), 1, (0, 1, 2), (0, 1, 2), 8), w_third[...])
        base = a3[o + 1]
        value = (base.astype(f32) + y.reshape(base.shape)).astype(bf16).astype(f32)
        put(p4, o, act(value, g4))

    for target, factor in ((0, k_b), (9, k_c)):
        p4[target] = (p4[target].astype(f32) * factor).astype(bf16)

    @pl.loop(0, 8)
    def _(o):
        patch = window(p4, o, 1, (0, 1, 2), (0, 1, 2), 8)
        colors = lax.dot_general(
            w_color[...], patch, (((1,), (1,)), ((), ())), preferred_element_type=f32
        )
        for k in range(out.shape[0]):
            out[k, pl.ds(o, 1)] = colors[k : k + 1]


def decode(tokens, keep, color, gains, own, other, rgb):
    count, cols = tokens.shape[:2]
    c1, c2, c3 = (2 * own[k].shape[-1] for k in (1, 3, 5))
    bf16 = jnp.bfloat16
    vmem, hbm = pl.BlockSpec(memory_space=pltpu.VMEM), pl.BlockSpec(memory_space=pltpu.HBM)
    wide = lambda w: pltpu.VMEM(w.shape[:-1] + (2 * w.shape[-1],), bf16)
    return pl.pallas_call(
        decode_kernel,
        out_shape=jax.ShapeDtypeStruct((rgb, 8, 8 * cols), jnp.float32),
        in_specs=[pl.BlockSpec(memory_space=pltpu.SMEM)] + [vmem] * 6 + [hbm] * 12,
        out_specs=vmem,
        scratch_shapes=[
            pltpu.VMEM((2 * count, 2, cols, c1), bf16),
            pltpu.VMEM((12, 4, cols, c1), bf16),
            pltpu.VMEM((12, 4, cols, c1), bf16),
            pltpu.VMEM((12, 4, cols, c2), bf16),
            pltpu.VMEM((14, 6, cols, c2), bf16),
            pltpu.VMEM((12, 6, cols, c2), bf16),
            pltpu.VMEM((12, 8, cols, c3), bf16),
            pltpu.VMEM((16, 10, cols, c3), bf16),
            pltpu.VMEM((10, 10, cols, c3), bf16),
            wide(own[0]), wide(own[1]), wide(own[2]), wide(own[3]),
            pltpu.VMEM((2,) + own[4].shape, bf16), pltpu.VMEM((2,) + own[5].shape, bf16),
            wide(own[4]), wide(own[5]),
            pltpu.SemaphoreType.DMA((2, 6)),
        ],
        compiler_params=pltpu.CompilerParams(vmem_limit_bytes=56 * 1024 * 1024),
    )(keep, tokens, color, *gains, *own, *other)


def body(
    latents,
    cond,
    embed,
    audio_table,
    audio_map,
    out_proj,
    tile_start,
    conv_input,
    conv_first,
    conv_second_up,
    conv_second,
    conv_third_up,
    conv_third,
    conv_color,
    gain_first,
    gain_second,
    gain_third,
    gain_color,
):
    latent = latents[0]
    tokens_here = latent.shape[0]
    frame_count = audio_table.shape[1]
    frames = jnp.repeat(audio_map, tokens_here // audio_map.shape[0])
    picks = (frames[:, None] == lax.broadcasted_iota(jnp.int32, (1, frame_count), 1)).astype(
        jnp.bfloat16
    )
    devices = lax.axis_size("seq")
    splits = max(devices // HEADS, 1)
    per_device = max(HEADS // devices, 1)
    groups = HEADS // per_device
    flat = lambda w: w.reshape(-1, w.shape[-1])
    taps = lambda w: w.reshape(9, *w.shape[2:])
    halves = (
        flat(conv_input), flat(conv_first), taps(conv_second_up),
        flat(conv_second), taps(conv_third_up), flat(conv_third),
    )
    handed, tokens, o_up2, o_up3, i_up2, i_up3, i_in, i_first, i_second, i_third = front(
        latent, cond[0], embed[0], audio_table[0], picks, out_proj[0], halves, splits, groups,
        per_device * HSIZE,
    )
    position = lax.axis_index("seq")
    block = position + jnp.arange(-2, 2)
    following = jnp.clip(block + 1, 0, devices - 1)
    inside = jnp.logical_and(block >= 0, block + 1 < devices)
    keep = jnp.where(jnp.logical_and(inside, tile_start[following] == 0), 1.0, 0.0)
    color = jnp.pad(flat(conv_color).T, ((0, 8 - conv_color.shape[3]), (0, 0)))
    gains = tuple(g[None] for g in (gain_first, gain_second, gain_third, gain_color))
    own = (halves[0], halves[1], o_up2, halves[3], o_up3, halves[5])
    other = (i_in, i_first, i_up2, i_second, i_up3, i_third)
    rgb = conv_color.shape[3]
    colors = decode(tokens, keep.astype(jnp.float32), color, gains, own, other, rgb)
    image = colors.reshape(rgb, 8, 8, -1).transpose(0, 1, 3, 2).reshape(rgb, 8, -1)
    return (handed[None], image)


def solution(mesh):
    in_specs = (
        P("section", ("replica", "seq"), None),
        P("section", None, ("replica", "seq"), None),
        P("section", None, None, None),
        P("section", "replica", None),
        P(("replica", "seq")),
        P("section", None, None),
        P("replica"),
        P(None, None, None, "section"),
        P(None, None, None, "section"),
        P(None, None, None, "section"),
        P(None, None, None, "section"),
        P(None, None, None, "section"),
        P(None, None, None, "section"),
        P(),
        P(),
        P(),
        P(),
        P(),
    )
    out_specs = (P("section", ("replica", "seq"), None), P(None, ("replica", "seq"), None))
    return jax.shard_map(body, mesh=mesh, in_specs=in_specs, out_specs=out_specs, check_vma=False)
```
